32 devices in a mesh: au: 4 (over y, x), vert: 8 (over z, core).
Axes of the slice: x: 2, y: 2, z: 4, core: 2. Of those that a mesh axis runs over, the one named last changes fastest.
Arguments:
- visibility: bfloat16 [2, 65536], P(None, ('au', 'vert')), may hold values from -6 to 6
- taps_u: bfloat16 [16, 65536], P(None, ('au', 'vert')), may hold values from 0.019897461 to 0.44921875
- taps_v: bfloat16 [16, 65536], P(None, ('au', 'vert')), may hold values from 0.019897461 to 0.44921875
- facet: int32 [65536, 1], P(('au', 'vert')), may hold values from 0 to 31; in each aligned block of 2048 rows (0 to 2047, 2048 to 4095, ...) at most 256 rows name the same one
- u_offset: int32 [65536], P(('au', 'vert')), may hold values from 0 to 2032
- v_offset: int32 [65536], P(('au', 'vert')), may hold values from 0 to 1008
Outputs:
- image: float32 [2, 8192, 8192], P(None, ('au', 'vert'))
The draws below stay inside these ranges and needn't reach their ends.
Inputs may be any that keep to these rules, and one draw needn't show every extreme that they name: Of the 2048 visibilities of one device at most 256 name the same facet, and some facet gets exactly 256 of some device's visibilities.
All inputs are finite; a program needn't handle non-finite values.
Results may differ from the reference program's by a relative error of at most 0.0058.
Values may be sent and summed in bfloat16 or wider, within the bound.
A program may use at most 128 MiB of HBM per device.

```python
import math
import jax
import jax.numpy as jnp
import numpy as np
from jax import lax

GRID = 8192
TAPS = 16
VIS_DEV = 2048
FACETS = 32
TU = 2048
TV = 1024
CAP = 256
VISIBILITIES = 65536
N_VERT = 8
DEVICES = 32


def touch_ends(result, own_key, smallest, high):
    spot = [jax.random.randint(jax.random.fold_in(own_key, axis), (), 0, length) for axis, length in enumerate(result.shape)]
    widest = result.shape.index(max(result.shape))
    neighbour = spot[:widest] + [(spot[widest] + 1) % result.shape[widest]] + spot[widest + 1:]
    return result.at[tuple(spot)].set(smallest).at[tuple(neighbour)].set(high)


def block_scale(stream_key, dims, split, least, largest):
    def one(position, shards_of):
        heights = jax.random.uniform(jax.random.fold_in(jax.random.fold_in(stream_key, 6), position), (shards_of,), jnp.float32, least / len(split), largest / len(split))
        return jnp.repeat(jnp.exp(heights), dims[position] // shards_of).reshape((-1,) + (1,) * (len(dims) - position - 1))

    level = one(*split[0])
    for cut in split[1:]:
        level = level * one(*cut)
    return level


def deal_out(stream_key, own, number, rows, count, top, bound, lean):
    sequence = jax.random.permutation(stream_key, count)
    crowded, ordinary = shares(count, rows * top, bound, lean, True), shares(count, rows * top, bound, lean, False)
    places = jnp.arange(count)

    def named(tallies, offset_by):
        used = int((tallies > 0).sum())
        fixed = max(1, used // 4)
        moved = fixed + (places - fixed + offset_by * (used - fixed)) % max(1, count - fixed)
        return jnp.zeros((count,), jnp.int32).at[sequence[jnp.where(places < fixed, places, moved)]].set(jnp.asarray(tallies, jnp.int32))

    tallies = jnp.where(number % 4 == 0, named(crowded, number // 4), named(ordinary, number - number // 4 - 1))
    mixed = jax.random.permutation(jax.random.fold_in(own, 3), count)
    donor, receiver = mixed[0:count // 2 * 2:2], mixed[1:count // 2 * 2:2]
    slack = jnp.minimum(tallies[donor] - 1, bound - tallies[receiver]) // 2
    slack = jnp.where((donor == sequence[0]) | (receiver == sequence[0]) | (tallies[receiver] == 0), 0, jnp.maximum(slack, 0))
    moved = jax.random.randint(jax.random.fold_in(own, 4), (count // 2,), 0, 1 << 20) % (slack + 1)
    tallies = tallies.at[donor].add(-moved).at[receiver].add(moved)
    items = jnp.searchsorted(jnp.cumsum(tallies), jnp.arange(rows * top), side="right").astype(jnp.int32)
    table = items.reshape(top, rows).T
    table = table[jax.random.permutation(jax.random.fold_in(own, 1), rows)]
    offset_by = jax.random.randint(jax.random.fold_in(own, 2), (rows, 1), 0, top)
    return jnp.take_along_axis(table, (jnp.arange(top)[None, :] + offset_by) % top, axis=1)


def shares(amount, total, bound, slope, full):
    loads = [(1 << 20) // math.isqrt(standing ** slope) + 1 for standing in range(1, amount + 1)]
    largest = bound if full else min(bound, max(-(-total // amount), total * loads[0] // sum(loads)))
    least = 1 if total - largest >= amount - 1 else 0
    given, spare = [largest] + [least] * (amount - 1), total - largest - least * (amount - 1)
    while spare > 0:
        candidates = [i for i in range(1, amount) if given[i] < largest] or [i for i in range(1, amount) if given[i] < bound]
        mass, left = sum([loads[i] for i in candidates]), spare
        for i in candidates:
            extra = min(bound - given[i], max(1, left * loads[i] // mass), spare)
            given[i] = given[i] + extra
            spare = spare - extra
    return np.array(given)


def bell_draw(key, shape, spread, limit, pieces=(), kind=jnp.bfloat16):
    result = spread * jax.random.normal(key, shape, jnp.float32)
    if pieces:
        result = result * block_scale(key, shape, pieces, -0.22, 0.18)
    return jnp.clip(result, -limit, limit).astype(kind)


def setup_inputs(seed: int = 0) -> dict:
    arg_keys = jax.random.split(jax.random.key(seed), 7)
    visibility = bell_draw(arg_keys[0], (2, VISIBILITIES), 1.0, 6.0, ((1, 32),))
    taps_u = jnp.clip(0.019897461 + 0.4293213 * jax.random.uniform(arg_keys[1], (TAPS, VISIBILITIES), jnp.float32) ** block_scale(arg_keys[1], (TAPS, VISIBILITIES), ((1, 32),), -0.2, 0.2), 0.019897461, 0.44921875).astype(jnp.bfloat16)
    taps_v = jnp.clip(0.019897461 + 0.4293213 * jax.random.uniform(arg_keys[2], (TAPS, VISIBILITIES), jnp.float32) ** block_scale(arg_keys[2], (TAPS, VISIBILITIES), ((1, 32),), -0.2, 0.2), 0.019897461, 0.44921875).astype(jnp.bfloat16)
    facet_keys = jax.random.split(jax.random.fold_in(arg_keys[3], 1), VISIBILITIES // VIS_DEV)
    facet_turns = jax.random.permutation(jax.random.fold_in(arg_keys[3], 3), VISIBILITIES // VIS_DEV)
    facet = jax.vmap(lambda own, number: deal_out(jax.random.fold_in(arg_keys[3], 2), own, number, VIS_DEV, FACETS, 1, CAP, 2))(facet_keys, facet_turns).reshape((VISIBILITIES, 1))
    u_offset = touch_ends(jax.random.randint(arg_keys[4], (VISIBILITIES,), 0, TU - TAPS + 1), jax.random.fold_in(arg_keys[4], 1), 0, TU - TAPS).astype(jnp.int32)
    v_offset = touch_ends(jax.random.randint(arg_keys[5], (VISIBILITIES,), 0, TV - TAPS + 1), jax.random.fold_in(arg_keys[5], 1), 0, TV - TAPS).astype(jnp.int32)
    return dict(visibility=visibility, taps_u=taps_u, taps_v=taps_v, facet=facet, u_offset=u_offset, v_offset=v_offset)


def reference(visibility, taps_u, taps_v, facet, u_offset, v_offset):
    tap = jnp.arange(TAPS, dtype=jnp.int32)
    vis_blocks = jnp.transpose(visibility.reshape(2, DEVICES, VIS_DEV), (1, 0, 2))
    tu_blocks = jnp.transpose(taps_u.reshape(TAPS, DEVICES, VIS_DEV), (1, 0, 2))
    tv_blocks = jnp.transpose(taps_v.reshape(TAPS, DEVICES, VIS_DEV), (1, 0, 2))
    facet_blocks = facet[:, 0].reshape(DEVICES, VIS_DEV)
    u_blocks = u_offset.reshape(DEVICES, VIS_DEV)
    v_blocks = v_offset.reshape(DEVICES, VIS_DEV)

    def accumulate(acc, items):
        vis, tu, tv, target, uo, vo = items
        kv = tv.astype(jnp.float32)
        weighted_re = lax.optimization_barrier((vis[0].astype(jnp.float32)[None, :] * kv).astype(jnp.bfloat16))
        weighted_im = lax.optimization_barrier((vis[1].astype(jnp.float32)[None, :] * kv).astype(jnp.bfloat16))
        ku = tu.astype(jnp.float32)
        rows = target // N_VERT * TU + uo
        cols = target % N_VERT * TV + vo
        row_cells = rows[None, :] + tap[:, None]
        col_cells = cols[None, :] + tap[:, None]
        value_re = ku[:, None, :] * weighted_re.astype(jnp.float32)[None, :, :]
        value_im = ku[:, None, :] * weighted_im.astype(jnp.float32)[None, :, :]
        row_index = jnp.broadcast_to(row_cells[:, None, :], value_re.shape)
        col_index = jnp.broadcast_to(col_cells[None, :, :], value_re.shape)
        acc = acc.at[0, row_index, col_index].add(value_re)
        acc = acc.at[1, row_index, col_index].add(value_im)
        return (acc, None)
    start = jnp.zeros((2, GRID, GRID), jnp.float32)
    grid, _ = lax.scan(accumulate, start, (vis_blocks, tu_blocks, tv_blocks, facet_blocks, u_blocks, v_blocks))
    plane = grid[0] + 1j * grid[1]
    picture = jnp.fft.ifft2(plane) * (float(GRID) * float(GRID) / jnp.sqrt(float(VISIBILITIES)))
    return jnp.stack([jnp.real(picture), jnp.imag(picture)]).astype(jnp.float32)
```

```python
import functools
import math

import jax
import jax.numpy as jnp
from jax import lax
from jax.experimental import pallas as pl
from jax.experimental.pallas import tpu as pltpu
from jax.sharding import PartitionSpec as P

GRID = 8192
TAPS = 16
LANES = 128
LOW = 64
STEP_BLOCKS = 4
FIELDS = 40
ROWS_OUT = 8


def phase_table(left, right, modulus):
    product = left[:, None] * right[None, :] % modulus
    angle = product.astype(jnp.float32) * (2.0 * math.pi / modulus)
    return jnp.cos(angle), jnp.sin(angle)


def rotated(taps, shift):
    tap = jnp.arange(TAPS, dtype=jnp.int32)[:, None]
    turned = jnp.zeros_like(taps)
    for t in range(TAPS):
        turned = turned + jnp.where((shift[None, :] + t) % TAPS == tap, taps[t : t + 1], 0)
    return turned


def tile_spread_kernel(first_ref, last_ref, pay_ref, low_ref, high_ref, acc_ref, *, tile, tiles, rows, period):
    source = pl.program_id(0)

    @pl.when(source == 0)
    def _():
        def clear(n, carry):
            acc_ref[n] = jnp.zeros(acc_ref.shape[1:], jnp.float32)
            return carry

        lax.fori_loop(0, acc_ref.shape[0], clear, 0)

    tap = lax.broadcasted_iota(jnp.int32, (TAPS, tile), 0).astype(jnp.float32)
    step_cells = STEP_BLOCKS * LANES

    def one_tile(t, carry):
        lanes = pl.ds(pl.multiple_of(t * tile, tile), tile)
        taps_v = pay_ref[0, 0:TAPS, lanes]
        taps_u = pay_ref[0, TAPS : 2 * TAPS, lanes]
        extra = pay_ref[0, 2 * TAPS : 2 * TAPS + 8, lanes].astype(jnp.float32)
        col_sixteenth = extra[0:1] * 16.0 + extra[1:2]
        col_low = extra[2:3]
        row_high = extra[3:4].astype(jnp.bfloat16)
        row_sixteenth = extra[4:5]
        row_low = extra[5:6]
        vis_re = extra[6:7].astype(jnp.bfloat16)
        vis_im = extra[7:8].astype(jnp.bfloat16)
        zero = jnp.zeros((), jnp.bfloat16)
        spot_u = (row_sixteenth + jnp.where(tap < row_low, 1.0, 0.0)).astype(jnp.bfloat16)
        band_u = jnp.concatenate(
            [jnp.where(spot_u == jnp.bfloat16(q), taps_u, zero) for q in range(LOW // TAPS + 1)], axis=0
        )
        low = jnp.dot(low_ref[...], band_u, preferred_element_type=jnp.float32)
        high_count = GRID // LOW
        number = lax.broadcasted_iota(jnp.int32, (high_count, tile), 0).astype(jnp.float32).astype(jnp.bfloat16)
        here = number == jnp.broadcast_to(row_high, (high_count, tile))
        picked = jnp.concatenate(
            [
                jnp.where(here, jnp.broadcast_to(vis_re, (high_count, tile)), zero),
                jnp.where(here, jnp.broadcast_to(vis_im, (high_count, tile)), zero),
            ],
            axis=0,
        )
        high = jnp.dot(high_ref[...], picked, preferred_element_type=jnp.float32)
        high_re, high_im = high[:period], high[period:]
        parts_re, parts_im = [], []
        for begin in range(0, rows, period):
            low_re = low[begin : begin + period]
            low_im = low[rows + begin : rows + begin + period]
            parts_re.append((low_re * high_re - low_im * high_im).astype(jnp.bfloat16))
            parts_im.append((low_re * high_im + low_im * high_re).astype(jnp.bfloat16))
        spread = jnp.concatenate(parts_re + parts_im, axis=0)
        spot_v = col_sixteenth + jnp.where(tap < col_low, 1.0, 0.0)

        def one_step(block, carry):
            base = (block * (step_cells // TAPS)).astype(jnp.float32)
            near = jnp.clip(spot_v - base, -1.0, step_cells / TAPS).astype(jnp.bfloat16)
            band_v = jnp.concatenate(
                [jnp.where(near == jnp.bfloat16(q), taps_v, zero) for q in range(step_cells // TAPS)], axis=0
            )
            out = lax.dot_general(spread, band_v, (((1,), (1,)), ((), ())), preferred_element_type=jnp.float32)
            for j in range(STEP_BLOCKS):
                acc_ref[block * STEP_BLOCKS + j] += out[:, j * LANES : (j + 1) * LANES]
            return carry

        place = source * tiles + t
        lax.fori_loop(first_ref[place], last_ref[place] + 1, one_step, 0)
        return carry

    lax.fori_loop(0, tiles, one_tile, 0)


def row_transform_kernel(plane_ref, first_ref, cos_ref, sin_ref, second_ref, out_ref):
    length = plane_ref.shape[0]
    stack = jnp.concatenate(
        [
            jnp.concatenate([plane_ref[:, part, m, :] for m in range(ROWS_OUT)], axis=1)
            for part in range(2)
        ],
        axis=0,
    ).astype(jnp.bfloat16)
    mid = jnp.dot(first_ref[...], stack, preferred_element_type=jnp.float32)
    cos, sin = cos_ref[...], sin_ref[...]
    rows = []
    for m in range(ROWS_OUT):
        re = mid[:length, m * LANES : (m + 1) * LANES]
        im = mid[length:, m * LANES : (m + 1) * LANES]
        rows.append(
            jnp.concatenate(
                [(re * cos - im * sin).astype(jnp.bfloat16), (re * sin + im * cos).astype(jnp.bfloat16)], axis=1
            )
        )
    turned = jnp.concatenate(rows, axis=0)
    out = lax.dot_general(second_ref[...], turned, (((1,), (1,)), ((), ())), preferred_element_type=jnp.float32)
    half = LANES // 2
    left = lax.broadcasted_iota(jnp.int32, (half, LANES), 1) < half
    for part in range(2):
        for pair in range(ROWS_OUT // 2):
            lanes = slice(pair * LANES, (pair + 1) * LANES)
            even = out[2 * part * half : (2 * part + 1) * half, lanes]
            odd = out[(2 * part + 1) * half : (2 * part + 2) * half, lanes]
            out_ref[part, 2 * pair] = jnp.where(left, even, pltpu.roll(odd, half, 1))
            out_ref[part, 2 * pair + 1] = jnp.where(left, pltpu.roll(even, half, 1), odd)


def stacked(cos, sin):
    return jnp.concatenate(
        [jnp.concatenate([cos, -sin], axis=1), jnp.concatenate([sin, cos], axis=1)], axis=0
    ).astype(jnp.bfloat16)


def on_device(visibility, taps_u, taps_v, facet, u_offset, v_offset):
    n_au = lax.axis_size("au")
    n_vert = lax.axis_size("vert")
    devices = n_au * n_vert
    count = visibility.shape[1]
    rows = GRID // devices
    own = lax.axis_index("au") * n_vert + lax.axis_index("vert")
    target = facet[:, 0]
    row = target // n_vert * (GRID // n_au) + u_offset
    col = target % n_vert * (GRID // n_vert) + v_offset
    key = col * count + jnp.arange(count, dtype=jnp.int32)
    rank = jnp.sum((key[:, None] < key[None, :]).astype(jnp.int32), axis=0)
    scalars = jnp.stack(
        [col // 256, col % 256 // TAPS, col % TAPS, row // LOW, row % LOW // TAPS, row % TAPS]
    ).astype(jnp.bfloat16)
    payload = jnp.concatenate(
        [rotated(taps_v, col % TAPS), rotated(taps_u, row % TAPS), scalars, visibility], axis=0
    )
    order = (rank[:, None] == jnp.arange(count, dtype=jnp.int32)[None, :]).astype(jnp.bfloat16)
    payload = jnp.dot(payload, order, preferred_element_type=jnp.float32).astype(jnp.bfloat16)
    gathered = lax.all_gather(payload, ("au", "vert"), axis=0)
    tile = math.gcd(count, 256)
    tiles = count // tile
    ends = gathered[:, 2 * TAPS : 2 * TAPS + 3, :].astype(jnp.int32)
    columns = (ends[:, 0] * 256 + ends[:, 1] * TAPS + ends[:, 2]).reshape(devices * tiles, tile)
    step_cells = STEP_BLOCKS * LANES
    first = jnp.min(columns, axis=1) // step_cells
    last = (jnp.max(columns, axis=1) + TAPS - 1) // step_cells

    k = own * rows + jnp.arange(rows, dtype=jnp.int32)
    low_cos, low_sin = phase_table(k, jnp.arange(LOW + TAPS, dtype=jnp.int32), GRID)
    low_table = jnp.concatenate([low_cos, low_sin], axis=0).astype(jnp.bfloat16)
    high_count = GRID // LOW
    period = min(rows, high_count)
    high_table = stacked(*phase_table(k[:period], jnp.arange(high_count, dtype=jnp.int32), high_count))
    blocks = GRID // LANES
    plane = pl.pallas_call(
        functools.partial(tile_spread_kernel, tile=tile, tiles=tiles, rows=rows, period=period),
        grid_spec=pltpu.PrefetchScalarGridSpec(
            num_scalar_prefetch=2,
            grid=(devices,),
            in_specs=[
                pl.BlockSpec((1, FIELDS, count), lambda s, *_: (s, 0, 0)),
                pl.BlockSpec(low_table.shape, lambda s, *_: (0, 0)),
                pl.BlockSpec(high_table.shape, lambda s, *_: (0, 0)),
            ],
            out_specs=pl.BlockSpec((blocks, 2 * rows, LANES), lambda s, *_: (0, 0, 0)),
        ),
        out_shape=jax.ShapeDtypeStruct((blocks, 2 * rows, LANES), jnp.float32),
        compiler_params=pltpu.CompilerParams(vmem_limit_bytes=60 * 1024 * 1024),
    )(first, last, gathered, low_table, high_table)

    a = jnp.arange(blocks, dtype=jnp.int32)
    b = jnp.arange(LANES, dtype=jnp.int32)
    first_table = stacked(*phase_table(a, a, blocks))
    cos, sin = phase_table(a, b, GRID)
    scale = 1.0 / math.sqrt(count * devices)
    mu = jnp.concatenate([jnp.arange(0, LANES, 2, dtype=jnp.int32), jnp.arange(1, LANES, 2, dtype=jnp.int32)])
    second_table = stacked(*phase_table(mu, b, LANES))
    whole = lambda shape: pl.BlockSpec(shape, lambda n: (0,) * len(shape))
    picture = pl.pallas_call(
        row_transform_kernel,
        grid=(rows // ROWS_OUT,),
        in_specs=[
            pl.BlockSpec((blocks, 2, ROWS_OUT, LANES), lambda n: (0, 0, n, 0)),
            whole(first_table.shape),
            whole(cos.shape),
            whole(sin.shape),
            whole(second_table.shape),
        ],
        out_specs=pl.BlockSpec((2, ROWS_OUT, blocks, LANES), lambda n: (0, n, 0, 0)),
        out_shape=jax.ShapeDtypeStruct((2, rows, blocks, LANES), jnp.float32),
        compiler_params=pltpu.CompilerParams(vmem_limit_bytes=48 * 1024 * 1024),
    )(plane.reshape(blocks, 2, rows, LANES), first_table, cos * scale, sin * scale, second_table)
    return picture.reshape(2, rows, GRID)


def solution(mesh):
    return jax.shard_map(
        on_device,
        mesh=mesh,
        in_specs=(
            P(None, ("au", "vert")),
            P(None, ("au", "vert")),
            P(None, ("au", "vert")),
            P(("au", "vert"), None),
            P(("au", "vert")),
            P(("au", "vert")),
        ),
        out_specs=P(None, ("au", "vert"), None),
        check_vma=False,
    )
```
